32 devices in a mesh: band: 4 (over y, core), sub: 8 (over z, x).
Axes of the slice: x: 2, y: 2, z: 4, core: 2. Of those that a mesh axis runs over, the one named last changes fastest.
Arguments:
- orientation: bfloat16 [16, 3, 4, 32768], P('band', None, None, 'sub'), may hold values from -1 to 1, as said below
- layup_id: int32 [4, 32768], P(None, 'sub'), may hold values from 0 to 7
- layup_table: int32 [8, 16], replicated, may hold values from 0 to 3
- grade_coefficients: float32 [4, 5], replicated, may hold values from -0.3 to 6, as said below
- connectivity: int32 [4, 131072], P(None, ('band', 'sub')), may hold values from 0 to 4351
- export_nodes: int32 [8192], P(('band', 'sub')), may hold values from 0 to 4095
- shift: float32 [5, 131072], P(None, ('band', 'sub')), may hold values from 0.2 to 2
- rhs: float32 [5, 131072], P(None, ('band', 'sub')), may hold values from -6 to 6
- coarse_inverse: float32 [4, 40, 40], replicated, may hold values from -1 to 1, as said below
Outputs:
- laminate_rows: float32 [18, 131072], P(None, ('band', 'sub'))
- solution_field: float32 [5, 131072], P(None, ('band', 'sub'))
- residual: float32 [5, 131072], P(None, ('band', 'sub'))
The draws below stay inside these ranges and needn't reach their ends.
Inputs may be any that keep to these rules, and one draw needn't show every extreme that they name: `layup_id`: each element's layup, one of 8. `layup_table`: fibre grade of a layer. `connectivity`: a slot below 4096 is an owned node of the element's device; slot 4096 + i is the ghost of the i-th entry of export_nodes of the device one band lower. `export_nodes`: indices of owned nodes. Valid in-plane orientation tensors: xx and yy non-negative, xx + yy at most 1, xy^2 at most xx yy. `grade_coefficients`: columns B1..B5 with B1 in [2, 6], B2 in [-0.3, 0.3], B3 in [0.5, 1.5], B4 and B5 in [0.5, 1]. `coarse_inverse`: each band's matrix is symmetric positive definite.
All inputs are finite; a program needn't handle non-finite values.
Results may differ from the reference program's by a relative error of at most 0.0003.
Values may be sent and summed in bfloat16 or wider, within the bound.
No kernel may reach another device: no remote copies, remote signals or barrier semaphores. Data moves between devices by JAX's collectives and lax.ppermute only.
A program may use at most 64 MiB of HBM per device.

```python
import math
import jax
import jax.numpy as jnp
from jax import lax

E_DEV = 4096
LAYERS = 16
GRADES = 4
LAYUPS = 8
ITERS = 3
NODE_DEV = 4096
HALO = 256
ESUB = 32768
E_TOT = 131072
N_TOT = 131072
NC = 40
N_BAND = 4
N_SUB = 8


def draw_orientation(key, part):
    shape = (LAYERS, N_BAND, ESUB)
    key_one, key_two, key_three = jax.random.split(key, 3)
    theta = jax.random.uniform(key_one, shape, jnp.float32, -math.pi, math.pi)
    align = jax.random.uniform(key_two, shape, jnp.float32, 0.3, 0.95)
    total = jax.random.uniform(key_three, shape, jnp.float32, 0.85, 1.0)
    cosine = jnp.cos(theta)
    sine = jnp.sin(theta)
    spread = 0.5 * (1.0 - align)
    comp_xx = total * (align * cosine * cosine + spread)
    comp_yy = total * (align * sine * sine + spread)
    comp_xy = total * align * cosine * sine
    return jnp.stack([comp_xx, comp_yy, comp_xy], axis=1).astype(jnp.bfloat16)


def draw_grade_coefficients(key, part):
    lows = jnp.array([2.0, -0.3, 0.5, 0.5, 0.5], jnp.float32)
    highs = jnp.array([6.0, 0.3, 1.5, 1.0, 1.0], jnp.float32)
    fraction = jax.random.uniform(key, (GRADES, 5), jnp.float32)
    return lows + fraction * (highs - lows)


def draw_coarse_inverse(key, part):
    key_one, key_two = jax.random.split(key)
    raw = jax.random.uniform(key_one, (N_BAND, NC, NC), jnp.float32, -1.0, 1.0) * (1.2 / NC)
    sym = 0.5 * (raw + jnp.swapaxes(raw, 1, 2))
    diag = 1.0 + jax.random.uniform(key_two, (N_BAND, NC), jnp.float32)
    rows = jnp.arange(NC)[:, None]
    cols = jnp.arange(NC)[None, :]
    eye = (rows == cols).astype(jnp.float32)
    return (sym * (1.0 - eye) + eye * diag[:, :, None]) * NODE_DEV ** (-0.5)


def set_ends(entries, own_key, least, top_value):
    longest = entries.shape.index(max(entries.shape))
    spots = []
    for shift in (0, 1):
        where = [jax.random.randint(jax.random.fold_in(own_key, axis), (), 0, length) for axis, length in enumerate(entries.shape)]
        where[longest] = (where[longest] + shift) % entries.shape[longest]
        spots.append(tuple(where))
    return entries.at[spots[0]].set(least).at[spots[1]].set(top_value)


def block_levels(key, dims, cuts, low, top_value):
    loudness = 1.0
    for position, blocks in cuts:
        heights = jax.random.uniform(jax.random.fold_in(jax.random.fold_in(key, 6), position), (blocks,), jnp.float32, low / len(cuts), top_value / len(cuts))
        loudness = loudness * jnp.repeat(jnp.exp(heights), dims[position] // blocks).reshape((-1,) + (1,) * (len(dims) - 1 - position))
    return loudness


def scatter_about(stream_key, dims, scale, limit, pieces=(), dtype=jnp.bfloat16):
    factor_of = block_levels(stream_key, dims, pieces, -0.22, 0.18) if pieces else 1.0
    values = jax.random.normal(stream_key, dims, jnp.float32) * scale * factor_of
    return jnp.minimum(jnp.maximum(values, -limit), limit).astype(dtype)


def setup_inputs(seed: int = 0) -> dict:
    splits = jax.random.split(jax.random.key(seed), 10)
    return {
        "orientation": draw_orientation(jax.random.fold_in(splits[9], 71), 0),
        "layup_id": set_ends(jax.random.randint(splits[1], (N_BAND, ESUB), 0, LAYUPS), jax.random.fold_in(splits[1], 1), 0, LAYUPS - 1).astype(jnp.int32),
        "layup_table": set_ends(jax.random.randint(splits[2], (LAYUPS, LAYERS), 0, GRADES), jax.random.fold_in(splits[2], 1), 0, GRADES - 1).astype(jnp.int32),
        "grade_coefficients": draw_grade_coefficients(jax.random.fold_in(splits[9], 71), 0),
        "connectivity": set_ends(jax.random.randint(splits[4], (4, E_TOT), 0, NODE_DEV + HALO), jax.random.fold_in(splits[4], 1), 0, (NODE_DEV + HALO) - 1).astype(jnp.int32),
        "export_nodes": set_ends(jax.random.randint(splits[5], (N_BAND * N_SUB * HALO,), 0, NODE_DEV), jax.random.fold_in(splits[5], 1), 0, NODE_DEV - 1).astype(jnp.int32),
        "shift": jnp.clip(jnp.exp(math.log(2.0) - 2.3025851 * jax.random.uniform(splits[6], (5, N_TOT), jnp.float32) ** block_levels(splits[6], (5, N_TOT), ((1, 32),), -0.2, 0.2)), 0.2, 2.0),
        "rhs": scatter_about(splits[7], (5, N_TOT), 1.0, 6.0, ((1, 32),), jnp.float32),
        "coarse_inverse": draw_coarse_inverse(jax.random.fold_in(splits[9], 71), 0),
    }


deriv_x = (-0.5, 0.5, 0.5, -0.5)
deriv_y = (-0.5, -0.5, 0.5, 0.5)
shear_factor = 5.0 / 6.0


def layer_stiffness(comp_xx, comp_yy, comp_xy, coefs):
    first, second, third, fourth, fifth = coefs[0], coefs[1], coefs[2], coefs[3], coefs[4]
    q_11 = first * comp_xx * comp_xx + (2.0 * second + 4.0 * third) * comp_xx + fourth + 2.0 * fifth
    q_12 = first * comp_xx * comp_yy + second * (comp_xx + comp_yy) + fourth
    q_22 = first * comp_yy * comp_yy + (2.0 * second + 4.0 * third) * comp_yy + fourth + 2.0 * fifth
    q_13 = comp_xy * (first * comp_xx + second + 2.0 * third)
    q_23 = comp_xy * (first * comp_yy + second + 2.0 * third)
    q_33 = first * comp_xy * comp_xy + third * (comp_xx + comp_yy) + fifth
    return jnp.stack([q_11, q_12, q_22, q_13, q_23, q_33], axis=0)


def apply_sym(comps, first, second, third):
    return (comps[0] * first + comps[1] * second + comps[3] * third,
            comps[1] * first + comps[2] * second + comps[4] * third,
            comps[3] * first + comps[4] * second + comps[5] * third)


def element_forces(view, laminate_rows, corners):
    gathered = [jnp.take(view, corners[a], axis=1) for a in range(4)]
    strain_a = 0.0
    strain_b = 0.0
    strain_c = 0.0
    curve_a = 0.0
    curve_b = 0.0
    curve_c = 0.0
    shear_a = 0.0
    shear_b = 0.0
    for a in range(4):
        node = gathered[a]
        strain_a = strain_a + deriv_x[a] * node[0]
        strain_b = strain_b + deriv_y[a] * node[1]
        strain_c = strain_c + deriv_y[a] * node[0] + deriv_x[a] * node[1]
        curve_a = curve_a + deriv_x[a] * node[3]
        curve_b = curve_b + deriv_y[a] * node[4]
        curve_c = curve_c + deriv_y[a] * node[3] + deriv_x[a] * node[4]
        shear_a = shear_a + deriv_x[a] * node[2] + 0.25 * node[3]
        shear_b = shear_b + deriv_y[a] * node[2] + 0.25 * node[4]
    membrane = laminate_rows[0:6]
    coupling = laminate_rows[6:12]
    bending = laminate_rows[12:18]
    mem_one = apply_sym(membrane, strain_a, strain_b, strain_c)
    mem_two = apply_sym(coupling, curve_a, curve_b, curve_c)
    bend_one = apply_sym(coupling, strain_a, strain_b, strain_c)
    bend_two = apply_sym(bending, curve_a, curve_b, curve_c)
    force_n = [mem_one[i] + mem_two[i] for i in range(3)]
    moment = [bend_one[i] + bend_two[i] for i in range(3)]
    stiff_s = shear_factor * membrane[5]
    shear_one = stiff_s * shear_a
    shear_two = stiff_s * shear_b
    summed = jnp.zeros(view.shape, jnp.float32)
    for a in range(4):
        force = jnp.stack([
            deriv_x[a] * force_n[0] + deriv_y[a] * force_n[2],
            deriv_y[a] * force_n[1] + deriv_x[a] * force_n[2],
            deriv_x[a] * shear_one + deriv_y[a] * shear_two,
            deriv_x[a] * moment[0] + deriv_y[a] * moment[2] + 0.25 * shear_one,
            deriv_y[a] * moment[1] + deriv_x[a] * moment[2] + 0.25 * shear_two], axis=0)
        summed = summed.at[:, corners[a]].add(force)
    return summed


def reference(orientation, layup_id, layup_table, grade_coefficients, connectivity, export_nodes, shift, rhs, coarse_inverse):
    devices = N_BAND * N_SUB
    orient = orientation.astype(jnp.float32).reshape(LAYERS, 3, E_TOT)
    ids = layup_id.reshape(E_TOT)
    thick = 1.0 / LAYERS
    membrane = jnp.zeros((6, E_TOT), jnp.float32)
    coupling = jnp.zeros((6, E_TOT), jnp.float32)
    bending = jnp.zeros((6, E_TOT), jnp.float32)
    for k in range(LAYERS):
        grade = layup_table[ids, k]
        coefs = grade_coefficients[grade].T
        stiff = layer_stiffness(orient[k, 0], orient[k, 1], orient[k, 2], coefs)
        centre = (k + 0.5) * thick - 0.5
        membrane = membrane + stiff * thick
        coupling = coupling + stiff * (thick * centre)
        bending = bending + stiff * (thick * centre * centre + thick ** 3 / 12.0)
    laminate_rows = jnp.concatenate([membrane, coupling, bending], axis=0)

    lam_dev = laminate_rows.reshape(18, devices, E_DEV).transpose(1, 0, 2)
    conn_dev = connectivity.reshape(4, devices, E_DEV).transpose(1, 0, 2)
    export_dev = export_nodes.reshape(devices, HALO)
    shift_dev = shift.reshape(5, devices, NODE_DEV).transpose(1, 0, 2)
    rhs_dev = rhs.reshape(5, devices, NODE_DEV).transpose(1, 0, 2)

    def operate(field):
        sent = jax.vmap(lambda vals, idx: jnp.take(vals, idx, axis=1))(field, export_dev)
        sent = sent.reshape(N_BAND, N_SUB, 5, HALO)
        ghost = jnp.concatenate([jnp.zeros((1, N_SUB, 5, HALO), jnp.float32), sent[:-1]], axis=0)
        view = jnp.concatenate([field, ghost.reshape(devices, 5, HALO)], axis=2)
        summed = jax.vmap(element_forces)(view, lam_dev, conn_dev)
        back = summed[:, :, NODE_DEV:].reshape(N_BAND, N_SUB, 5, HALO)
        recv = jnp.concatenate([back[1:], jnp.zeros((1, N_SUB, 5, HALO), jnp.float32)], axis=0)
        owned = jax.vmap(lambda vals, idx, extra: vals.at[:, idx].add(extra))(
            summed[:, :, :NODE_DEV], export_dev, recv.reshape(devices, 5, HALO))
        return owned + shift_dev * field

    def precondition(resid):
        sums = jnp.sum(resid, axis=2).reshape(N_BAND, N_SUB * 5)
        coefs = jnp.einsum('bij,bj->bi', coarse_inverse, sums, precision=lax.Precision.HIGHEST)
        return resid + coefs.reshape(devices, 5)[:, :, None]

    solution = jnp.zeros_like(rhs_dev)
    resid = rhs_dev
    precond = precondition(resid)
    direction = precond
    rz_now = jnp.sum(resid * precond)
    for step in range(ITERS):
        image = operate(direction)
        alpha = rz_now / jnp.sum(direction * image)
        solution = solution + alpha * direction
        resid = resid - alpha * image
        precond = precondition(resid)
        rz_next = jnp.sum(resid * precond)
        direction = precond + (rz_next / rz_now) * direction
        rz_now = rz_next
    solution_field = solution.transpose(1, 0, 2).reshape(5, N_TOT)
    residual = resid.transpose(1, 0, 2).reshape(5, N_TOT)
    return laminate_rows, solution_field, residual
```

```python
import jax
import jax.numpy as jnp
from jax import lax
from jax.experimental import pallas as pl
from jax.experimental.pallas import tpu as pltpu
from jax.sharding import PartitionSpec as P

ITERS = 3
LANES = 128
WIDE = 256
SPLITS = 2

deriv_x = (-0.5, 0.5, 0.5, -0.5)
deriv_y = (-0.5, -0.5, 0.5, 0.5)
shear_factor = 5.0 / 6.0


def lane_gather(table, index):
    dims = lax.GatherDimensionNumbers(
        offset_dims=(),
        collapsed_slice_dims=(1,),
        start_index_map=(1,),
        operand_batching_dims=(0,),
        start_indices_batching_dims=(0,),
    )
    return lax.gather(
        table, index[..., None], dims, slice_sizes=(1, 1), mode=lax.GatherScatterMode.PROMISE_IN_BOUNDS
    )


def total(value):
    return jnp.sum(jnp.sum(value, axis=0, keepdims=True), axis=1, keepdims=True)


def split_terms(value):
    high = value.astype(jnp.bfloat16).astype(jnp.float32)
    return high, value - high


def contract_last(left, right):
    return lax.dot_general(
        left, right, (((1,), (1,)), ((), ())), preferred_element_type=jnp.float32
    )


def iota_rows(start, rows=16):
    return (lax.broadcasted_iota(jnp.int32, (rows, LANES), 0) + start).astype(jnp.float32).astype(jnp.bfloat16)


def wide_rows(row):
    return jnp.broadcast_to(row, (16, LANES)).astype(jnp.bfloat16)


def onehot(row, start):
    return jnp.where(row == iota_rows(start), jnp.bfloat16(1), jnp.bfloat16(0))


def place_row(block_shape, band, sub, values, row):
    rows = lax.broadcasted_iota(jnp.int32, block_shape, 0)
    lanes = lax.broadcasted_iota(jnp.int32, block_shape, 1)
    block = jnp.zeros(block_shape, jnp.float32)
    for k in range(5):
        block = jnp.where((rows == row) & (lanes == sub * 5 + k), values[k], block)
    return block


def place_scalars(block_shape, row, values):
    rows = lax.broadcasted_iota(jnp.int32, block_shape, 0)
    lanes = lax.broadcasted_iota(jnp.int32, block_shape, 1)
    block = jnp.zeros(block_shape, jnp.float32)
    for k, value in enumerate(values):
        block = jnp.where((rows == row) & (lanes == k), value, block)
    return block


def coarse_values(inverse_ref, modal_ref, band, sub):
    count = inverse_ref.shape[2]
    product = inverse_ref[band] * modal_ref[pl.ds(band, 1), 0:count]
    rows = lax.broadcasted_iota(jnp.int32, product.shape, 0)
    return [total(jnp.where(rows == sub * 5 + k, product, 0.0)) for k in range(5)]


def prepare_kernel(place_ref, rhs_ref, shift_ref, conn_ref, export_ref,
                   resid_ref, shift_out, conn_out, sent_ref, block_ref):
    band = place_ref[0]
    sub = place_ref[1]
    hi_rows = resid_ref.shape[1]
    for c in range(5):
        for h in range(hi_rows):
            resid_ref[c, h : h + 1, :] = rhs_ref[c : c + 1, h * WIDE : (h + 1) * WIDE]
            shift_out[c, h : h + 1, :] = shift_ref[c : c + 1, h * WIDE : (h + 1) * WIDE]
    for a in range(4):
        for h in range(conn_out.shape[1]):
            conn_out[a, h : h + 1, :] = conn_ref[a : a + 1, h * LANES : (h + 1) * LANES]
    gather_export(resid_ref, export_ref, sent_ref)
    modal = [total(resid_ref[c]) for c in range(5)]
    block_ref[...] = jnp.broadcast_to(
        place_row(block_ref.shape[1:], band, sub, modal, band)[None], block_ref.shape
    )


def gather_export(field_ref, export_ref, out_ref):
    halo = export_ref.shape[1]
    out_ref[...] = jnp.zeros(out_ref.shape, jnp.float32)
    parts = halo // LANES
    index = jnp.concatenate(
        [export_ref[:, g * LANES : (g + 1) * LANES] for g in range(parts)]
        + [jnp.zeros((8 - parts, LANES), jnp.int32)], axis=0)
    row = index >> 7
    low = index & 127
    found = [jnp.zeros((8, LANES), jnp.float32)] * 5
    for h in range(2 * field_ref.shape[1]):
        mask = row == h
        for c in range(5):
            table = jnp.broadcast_to(
                field_ref[c, h // 2 : h // 2 + 1, (h % 2) * LANES : (h % 2 + 1) * LANES], (8, LANES))
            found[c] = jnp.where(mask, lane_gather(table, low), found[c])
    for c in range(5):
        for g in range(parts):
            out_ref[c : c + 1, g * LANES : (g + 1) * LANES] = found[c][g : g + 1, :]


def laminate_kernel(place_ref, orient_ref, ids_ref, table_ref, rows_ref, dense_ref):
    band = place_ref[0]
    bands, _, per, count = orient_ref.shape
    layers = bands * per
    layups = table_ref.shape[1]
    thick = 1.0 / layers
    level = lax.broadcasted_iota(jnp.int32, (layers, LANES), 0).astype(jnp.float32)
    centre = (level + 0.5) * thick - 0.5
    square = centre * centre + thick * thick / 12.0
    table = table_ref[...]

    def step(j, carry):
        lanes = pl.ds(pl.multiple_of(j * LANES, LANES), LANES)
        choices = ids_ref[:, lanes]
        chosen = lax.broadcasted_iota(jnp.int32, choices.shape, 0) == band
        ids = jnp.sum(jnp.where(chosen, choices, 0), axis=0, keepdims=True)
        picks = (lax.broadcasted_iota(jnp.int32, (layups, LANES), 0) == ids).astype(jnp.float32)
        coefs = lax.dot_general(table, picks, (((1,), (0,)), ((), ())),
                                precision=lax.Precision.HIGHEST, preferred_element_type=jnp.float32)
        first, double, ends, second, fourth, single, third, fifth = [
            coefs[q * layers : (q + 1) * layers] for q in range(8)]
        comp_xx, comp_yy, comp_xy = [
            jnp.concatenate([orient_ref[b, m, :, lanes].astype(jnp.float32) for b in range(bands)], axis=0)
            for m in range(3)]
        scaled_x = first * comp_xx
        scaled_y = first * comp_yy
        both = comp_xx + comp_yy
        stiff = (
            (scaled_x + double) * comp_xx + ends,
            scaled_x * comp_yy + second * both + fourth,
            (scaled_y + double) * comp_yy + ends,
            comp_xy * (scaled_x + single),
            comp_xy * (scaled_y + single),
            first * comp_xy * comp_xy + third * both + fifth,
        )
        for q in range(6):
            sums = (
                jnp.sum(stiff[q], axis=0, keepdims=True) * thick,
                jnp.sum(stiff[q] * centre, axis=0, keepdims=True) * thick,
                jnp.sum(stiff[q] * square, axis=0, keepdims=True) * thick,
            )
            for m in range(3):
                row = m * 6 + q
                rows_ref[row : row + 1, lanes] = sums[m]
                dense_ref[row, pl.ds(j, 1), :] = sums[m]
        return carry

    lax.fori_loop(0, count // LANES, step, 0)


def matvec(z_ref, ghost_ref, lam_ref, conn_ref, force_ref, acc_ref, left_ref, right_ref):
    hi_rows = z_ref.shape[1]
    tables = 2 * hi_rows
    ghost_parts = ghost_ref.shape[1] // LANES
    blocks = conn_ref.shape[1] // 8
    elem_rows = conn_ref.shape[1]

    def block_step(block, energy):
        rows = pl.ds(pl.multiple_of(block * 8, 8), 8)
        index = [conn_ref[a, rows, :] for a in range(4)]
        row = [value >> 7 for value in index]
        low = [value & 127 for value in index]
        node = [[jnp.zeros((8, LANES), jnp.float32)] * 5 for _ in range(4)]
        for h in range(tables + ghost_parts):
            masks = [value == h for value in row]
            for c in range(5):
                if h < tables:
                    source = z_ref[c, h // 2 : h // 2 + 1, (h % 2) * LANES : (h % 2 + 1) * LANES]
                else:
                    g = h - tables
                    source = ghost_ref[c : c + 1, g * LANES : (g + 1) * LANES]
                table = jnp.broadcast_to(source, (8, LANES))
                for a in range(4):
                    node[a][c] = jnp.where(masks[a], lane_gather(table, low[a]), node[a][c])

        def along_x(c):
            return 0.5 * ((node[1][c] - node[0][c]) + (node[2][c] - node[3][c]))

        def along_y(c):
            return 0.5 * ((node[2][c] - node[1][c]) + (node[3][c] - node[0][c]))

        def mean(c):
            return 0.25 * ((node[0][c] + node[1][c]) + (node[2][c] + node[3][c]))

        strain = (along_x(0), along_y(1), along_y(0) + along_x(1))
        curve = (along_x(3), along_y(4), along_y(3) + along_x(4))
        shear_one = along_x(2) + mean(3)
        shear_two = along_y(2) + mean(4)
        lam = [lam_ref[q, rows, :] for q in range(18)]

        def apply_sym(comps, vec):
            return (
                comps[0] * vec[0] + comps[1] * vec[1] + comps[3] * vec[2],
                comps[1] * vec[0] + comps[2] * vec[1] + comps[4] * vec[2],
                comps[3] * vec[0] + comps[4] * vec[1] + comps[5] * vec[2],
            )

        mem = apply_sym(lam[0:6], strain)
        mix = apply_sym(lam[6:12], curve)
        mix_two = apply_sym(lam[6:12], strain)
        bend = apply_sym(lam[12:18], curve)
        force = [mem[i] + mix[i] for i in range(3)]
        moment = [mix_two[i] + bend[i] for i in range(3)]
        stiff_s = shear_factor * lam[5]
        cut_one = stiff_s * shear_one
        cut_two = stiff_s * shear_two
        energy = energy + (force[0] * strain[0] + force[1] * strain[1] + force[2] * strain[2])
        energy = energy + (moment[0] * curve[0] + moment[1] * curve[1] + moment[2] * curve[2])
        energy = energy + (cut_one * shear_one + cut_two * shear_two)
        for a in range(4):
            values = (
                deriv_x[a] * force[0] + deriv_y[a] * force[2],
                deriv_y[a] * force[1] + deriv_x[a] * force[2],
                deriv_x[a] * cut_one + deriv_y[a] * cut_two,
                deriv_x[a] * moment[0] + deriv_y[a] * moment[2] + 0.25 * cut_one,
                deriv_y[a] * moment[1] + deriv_x[a] * moment[2] + 0.25 * cut_two,
            )
            base = (a * elem_rows + block * 8) * 16
            for c in range(5):
                high, rest = split_terms(values[c])
                force_ref[pl.ds(base + c, 8, stride=16), :] = high
                force_ref[pl.ds(base + 5 + c, 8, stride=16), :] = rest
        return energy

    energy = lax.fori_loop(0, blocks, block_step, jnp.zeros((8, LANES), jnp.float32))

    acc_ref[...] = jnp.zeros(acc_ref.shape, jnp.float32)

    def scatter_step(group, carry):
        corner = group // blocks
        block = group % blocks
        index = conn_ref[corner, pl.ds(pl.multiple_of(block * 8, 8), 8), :]
        high = (index >> 8).astype(jnp.float32)
        low = (index & 255).astype(jnp.float32)
        for q in range(8):
            cols = slice(q * LANES, (q + 1) * LANES)
            high_row = wide_rows(high[q : q + 1, :])
            low_row = wide_rows(low[q : q + 1, :])
            pick = onehot(high_row, 0)
            start = pl.multiple_of((group * 8 + q) * 16, 16)
            tile = force_ref[pl.ds(start, 16), :]
            for k in range(5 * SPLITS):
                left_ref[k * 16 : (k + 1) * 16, cols] = pick * wide_rows(tile[k : k + 1, :])
            on_ghost = jnp.where(high_row == jnp.bfloat16(hi_rows), jnp.bfloat16(1), jnp.bfloat16(0))
            left_ref[5 * SPLITS * 16 : 5 * SPLITS * 16 + 16, cols] = on_ghost * tile.astype(jnp.bfloat16)
            for j in range(WIDE // 16):
                right_ref[j * 16 : (j + 1) * 16, cols] = onehot(low_row, j * 16)
        acc_ref[...] += contract_last(left_ref[...], right_ref[...])
        return carry

    lax.fori_loop(0, 4 * blocks, scatter_step, 0)
    return energy


def scatter_back(back_ref, export_ref, live, left_ref, right_ref):
    halo = export_ref.shape[1]
    for q in range(halo // LANES):
        cols = slice(q * LANES, (q + 1) * LANES)
        index = export_ref[:, cols]
        high_row = wide_rows((index >> 8).astype(jnp.float32))
        low_row = wide_rows((index & 255).astype(jnp.float32))
        pick = onehot(high_row, 0)
        for c in range(5):
            terms = split_terms(jnp.where(live, back_ref[c : c + 1, cols], 0.0))
            for t in range(2):
                k = t * 5 + c
                left_ref[k * 16 : (k + 1) * 16, cols] = pick * wide_rows(terms[t])
        for j in range(WIDE // 16):
            right_ref[j * 16 : (j + 1) * 16, cols] = onehot(low_row, j * 16)
    summed = contract_last(left_ref[0 : 160, 0:halo], right_ref[:, 0:halo])
    return [summed[c * 16 : (c + 1) * 16] + summed[(5 + c) * 16 : (6 + c) * 16] for c in range(5)]


def finish_matvec(place, refs):
    band, sub, bands = place
    (z_ref, resid_ref, image_ref, shift_ref, acc_ref, energy, export_ref,
     own_ref, ghost_sum_ref, sent_ref, block_ref) = refs
    modal = []
    square = jnp.zeros((16, WIDE), jnp.float32)
    with_resid = jnp.zeros((16, WIDE), jnp.float32)
    with_image = jnp.zeros((16, WIDE), jnp.float32)
    for c in range(5):
        z = z_ref[c]
        held = shift_ref[c] * z
        square = square + held * z
        with_resid = with_resid + resid_ref[c] * z
        if image_ref is not None:
            with_image = with_image + image_ref[c] * z
        value = acc_ref[c * 16 : (c + 1) * 16] + acc_ref[(5 + c) * 16 : (6 + c) * 16] + held
        own_ref[c] = value
        modal.append(total(value))
    ghost = acc_ref[160:165] + acc_ref[165:170]
    ghost_sum_ref[...] = jnp.concatenate([ghost, jnp.zeros((3, ghost.shape[1]), jnp.float32)], axis=0)
    lower = [total(ghost_sum_ref[c : c + 1, :]) for c in range(5)]
    if sent_ref is not None:
        gather_export(own_ref, export_ref, sent_ref)
    scalars = [total(energy) + total(square), total(with_image), total(with_resid)]
    shape = block_ref.shape[1:]
    block = place_row(shape, band, sub, modal, band)
    block = block + jnp.where(band > 0, place_row(shape, band, sub, lower, band - 1), 0.0)
    block = block + place_scalars(shape, bands, scalars)
    block_ref[...] = jnp.broadcast_to(block[None], block_ref.shape)


def begin_kernel(place_ref, blocks_ref, ghost_in, partner_ref, resid_ref, shift_ref, inverse_ref, lam_ref, conn_ref,
                 export_ref,
                 z_ref, own_ref, ghost_sum_ref, sent_ref, block_ref, ghost_resid_ref, state_ref, same_ref,
                 ghost_ref, force_ref, acc_ref, left_ref, right_ref):
    band, sub = place_ref[0], place_ref[1]
    bands = inverse_ref.shape[0]
    state_ref[...] = jnp.zeros(state_ref.shape, jnp.float32)
    state_ref[0] = jnp.sum(blocks_ref[...], axis=0)
    mine = coarse_values(inverse_ref, state_ref.at[0], band, sub)
    lower = coarse_values(inverse_ref, state_ref.at[0], jnp.maximum(band - 1, 0), sub)
    for c in range(5):
        z_ref[c] = resid_ref[c] + mine[c]
    ghost_resid_ref[...] = ghost_in[...]
    ghost_ref[...] = jnp.zeros(ghost_ref.shape, jnp.float32)
    for c in range(5):
        value = ghost_in[c : c + 1, :] + lower[c]
        ghost_ref[c : c + 1, :] = jnp.where(band > 0, value, 0.0)
    halo = partner_ref.shape[1]
    spread = jnp.broadcast_to(partner_ref[...].astype(jnp.float32), (halo, halo))
    same_ref[...] = jnp.where(spread == spread.T, 1.0, 0.0).astype(jnp.bfloat16)
    energy = matvec(z_ref, ghost_ref, lam_ref, conn_ref, force_ref, acc_ref, left_ref, right_ref)
    finish_matvec((band, sub, bands), (z_ref, resid_ref, None, shift_ref, acc_ref, energy, export_ref,
                                       own_ref, ghost_sum_ref, sent_ref, block_ref))


def step_scalars(blocks_ref, state_ref, bands, first):
    block = jnp.sum(blocks_ref[...], axis=0)
    energy = block[bands : bands + 1, 0:1]
    cross = block[bands : bands + 1, 1:2]
    gamma = block[bands : bands + 1, 2:3]
    if first:
        return block, gamma, jnp.zeros_like(gamma), energy, gamma / energy
    beta = gamma / state_ref[2, 0:1, 0:1]
    curve = energy + 2.0 * beta * cross + beta * beta * state_ref[2, 1:2, 0:1]
    return block, gamma, beta, curve, gamma / curve


def advance_kernel(first, send, *refs):
    it = iter(refs)
    place_ref, blocks_ref, back_ref, got_ref = next(it), next(it), next(it), next(it)
    own_in, ghost_sum_in, z_in, resid_in, state_in, ghost_resid_in, same_ref = (next(it) for _ in range(7))
    if not first:
        dir_in, image_in, field_in, ghost_image_in = (next(it) for _ in range(4))
    shift_ref, inverse_ref, lam_ref, conn_ref, export_ref = (next(it) for _ in range(5))
    z_ref, resid_ref, dir_ref, image_ref, field_ref, own_ref, ghost_sum_ref = (next(it) for _ in range(7))
    sent_ref = next(it) if send else None
    block_ref, ghost_resid_ref, ghost_image_ref, state_ref = (next(it) for _ in range(4))
    ghost_ref, force_ref, acc_ref, left_ref, right_ref = (next(it) for _ in range(5))
    band, sub = place_ref[0], place_ref[1]
    bands = inverse_ref.shape[0]
    block, gamma, beta, curve, alpha = step_scalars(blocks_ref, state_in, bands, first)
    modal_image = block if first else block + beta * state_in[1]
    state_ref[1] = modal_image
    state_ref[0] = state_in[0] - alpha * modal_image
    state_ref[2] = jnp.zeros(state_ref.shape[1:], jnp.float32)
    state_ref[2, 0:1, :] = jnp.broadcast_to(gamma, (1, state_ref.shape[2]))
    state_ref[2, 1:2, :] = jnp.broadcast_to(curve, (1, state_ref.shape[2]))
    mine = coarse_values(inverse_ref, state_ref.at[0], band, sub)
    lower = coarse_values(inverse_ref, state_ref.at[0], jnp.maximum(band - 1, 0), sub)
    back = scatter_back(back_ref, export_ref, band < bands - 1, left_ref, right_ref)
    for c in range(5):
        image = own_in[c] + back[c]
        direction = z_in[c]
        if not first:
            image = image + beta * image_in[c]
            direction = direction + beta * dir_in[c]
        image_ref[c] = image
        dir_ref[c] = direction
        moved = alpha * direction
        field_ref[c] = moved if first else field_in[c] + moved
        resid = resid_in[c] - alpha * image
        resid_ref[c] = resid
        z_ref[c] = resid + mine[c]
    terms = split_terms(ghost_sum_in[...])
    same = same_ref[...]
    shared = sum(jnp.dot(term.astype(jnp.bfloat16), same, preferred_element_type=jnp.float32) for term in terms)
    ghost_image = got_ref[...] + shared
    if not first:
        ghost_image = ghost_image + beta * ghost_image_in[...]
    ghost_image_ref[...] = ghost_image
    ghost_resid = ghost_resid_in[...] - alpha * ghost_image
    ghost_resid_ref[...] = ghost_resid
    ghost_ref[...] = jnp.zeros(ghost_ref.shape, jnp.float32)
    for c in range(5):
        value = ghost_resid_ref[c : c + 1, :] + lower[c]
        ghost_ref[c : c + 1, :] = jnp.where(band > 0, value, 0.0)
    energy = matvec(z_ref, ghost_ref, lam_ref, conn_ref, force_ref, acc_ref, left_ref, right_ref)
    finish_matvec((band, sub, bands), (z_ref, resid_ref, image_ref, shift_ref, acc_ref, energy, export_ref,
                                       own_ref, ghost_sum_ref, sent_ref, block_ref))


def close_kernel(place_ref, blocks_ref, back_ref, own_in, z_in, resid_in, state_in, dir_in, image_in, field_in,
                 export_ref, field_ref, resid_ref, left_ref, right_ref):
    band = place_ref[0]
    bands = place_ref[2]
    last = blocks_ref.shape[1] - 1
    block, gamma, beta, curve, alpha = step_scalars(blocks_ref, state_in, last, False)
    back = scatter_back(back_ref, export_ref, band < bands - 1, left_ref, right_ref)
    for c in range(5):
        image = own_in[c] + back[c] + beta * image_in[c]
        direction = z_in[c] + beta * dir_in[c]
        field = field_in[c] + alpha * direction
        resid = resid_in[c] - alpha * image
        for h in range(field.shape[0]):
            field_ref[c : c + 1, h * WIDE : (h + 1) * WIDE] = field[h : h + 1, :]
            resid_ref[c : c + 1, h * WIDE : (h + 1) * WIDE] = resid[h : h + 1, :]


def call(kernel, name, outs, scratch, *args):
    shapes = [jax.ShapeDtypeStruct(*out) for out in outs]
    specs = [pl.BlockSpec(memory_space=pltpu.SMEM)] + [
        pl.BlockSpec(memory_space=pltpu.VMEM) for _ in args[1:]]
    return pl.pallas_call(
        kernel,
        out_shape=shapes,
        in_specs=specs,
        out_specs=[pl.BlockSpec(memory_space=pltpu.VMEM) for _ in outs],
        scratch_shapes=scratch,
        name=name,
    )(*args)


def ring(value, axis, step):
    count = lax.axis_size(axis)
    return lax.ppermute(value, axis, [(j, (j + step) % count) for j in range(count)])


def shards(
    orientation,
    layup_id,
    layup_table,
    grade_coefficients,
    connectivity,
    export_nodes,
    shift,
    rhs,
    coarse_inverse,
):
    f32 = jnp.float32
    bands = lax.axis_size("band")
    devices = bands * lax.axis_size("sub")
    nodes = rhs.shape[1]
    elements = connectivity.shape[1]
    halo = export_nodes.shape[0]
    hi_rows = nodes // WIDE
    coarse = coarse_inverse.shape[1]
    lanes = -(-coarse // LANES) * LANES
    block_shape = (devices, bands + 1, lanes)
    field_shape = (5, hi_rows, WIDE)
    place = jnp.stack([lax.axis_index("band"), lax.axis_index("sub"), jnp.int32(bands)]).astype(jnp.int32)

    packed = orientation.transpose(2, 1, 0, 3)
    layers = lax.all_to_all(packed, "band", 0, 0, tiled=True)

    export = export_nodes.reshape(1, halo)
    resid, shift_d, conn, sent, block = call(
        prepare_kernel, "prepare",
        [(field_shape, f32), (field_shape, f32), ((4, elements // LANES, LANES), jnp.int32),
         ((8, halo), f32), (block_shape, f32)],
        [], place, rhs, shift, connectivity, export)
    got = ring(sent, "band", 1)
    partner = ring(export, "band", 1)
    blocks = lax.all_to_all(block, ("band", "sub"), 0, 0, tiled=True)

    per_layer = grade_coefficients[layup_table]
    b1, b2, b3, b4, b5 = (per_layer[:, :, q] for q in range(5))
    table = jnp.concatenate(
        [b1, 2.0 * b2 + 4.0 * b3, b4 + 2.0 * b5, b2, b4, b2 + 2.0 * b3, b3, b5], axis=1).T
    lam_rows, lam = call(
        laminate_kernel, "laminate",
        [((18, elements), f32), ((18, elements // LANES, LANES), f32)],
        [], place, layers, layup_id, table)

    rows = 5 * SPLITS * 16 + 16
    scratch = [
        pltpu.VMEM((8, halo), f32),
        pltpu.VMEM((4 * (elements // LANES) * 16, LANES), f32),
        pltpu.VMEM((rows, WIDE), f32),
        pltpu.VMEM((rows, 8 * LANES), jnp.bfloat16),
        pltpu.VMEM((WIDE, 8 * LANES), jnp.bfloat16),
    ]
    state_shape = (3, bands + 1, lanes)
    field_out = (field_shape, f32)
    ghost_out = ((8, halo), f32)
    z, own, ghost_sum, sent, block, ghost_resid, state, same = call(
        begin_kernel, "begin",
        [field_out, field_out, ghost_out, ghost_out, (block_shape, f32), ghost_out, (state_shape, f32),
         ((halo, halo), jnp.bfloat16)],
        scratch, place, blocks, got, partner, resid, shift_d, coarse_inverse, lam, conn, export)

    direction = image = field = ghost_image = None
    for step in range(ITERS - 1):
        first = step == 0
        send = step < ITERS - 2
        back = ring(ghost_sum, "band", -1)
        got = ring(sent, "band", 1)
        blocks = lax.all_to_all(block, ("band", "sub"), 0, 0, tiled=True)
        past = [] if first else [direction, image, field, ghost_image]
        outs = [field_out] * 6 + [ghost_out] + ([ghost_out] if send else []) + [
            (block_shape, f32), ghost_out, ghost_out, (state_shape, f32)]
        got_all = call(
            lambda *refs, first=first, send=send: advance_kernel(first, send, *refs), f"advance{step}",
            outs, scratch, place, blocks, back, got, own, ghost_sum, z, resid, state, ghost_resid, same,
            *past, shift_d, coarse_inverse, lam, conn, export)
        z, resid, direction, image, field, own, ghost_sum = got_all[:7]
        sent = got_all[7] if send else None
        block, ghost_resid, ghost_image, state = got_all[-4:]

    back = ring(ghost_sum, "band", -1)
    blocks = lax.all_to_all(block, ("band", "sub"), 0, 0, tiled=True)
    out_field, out_resid = call(
        close_kernel, "close", [((5, nodes), f32), ((5, nodes), f32)],
        scratch[3:], place, blocks, back, own, z, resid, state, direction, image, field, export)
    return lam_rows, out_field, out_resid


def solution(mesh):
    placed = (
        P("band", None, None, "sub"),
        P(None, "sub"),
        P(),
        P(),
        P(None, ("band", "sub")),
        P(("band", "sub")),
        P(None, ("band", "sub")),
        P(None, ("band", "sub")),
        P(),
    )
    return jax.shard_map(
        shards,
        mesh=mesh,
        in_specs=placed,
        out_specs=(P(None, ("band", "sub")), P(None, ("band", "sub")), P(None, ("band", "sub"))),
        check_vma=False,
    )
```

```python
import functools

import jax
import jax.numpy as jnp
from jax import lax
from jax.experimental import pallas as pl
from jax.experimental.pallas import tpu as pltpu
from jax.sharding import PartitionSpec as P

ITERS = 3
LANES = 128
WIDE = 256
SPLITS = 2
GRANT = 20 * 1024 * 1024

deriv_x = (-0.5, 0.5, 0.5, -0.5)
deriv_y = (-0.5, -0.5, 0.5, 0.5)
shear_factor = 5.0 / 6.0


def lane_gather(table, index):
    dims = lax.GatherDimensionNumbers(
        offset_dims=(),
        collapsed_slice_dims=(1,),
        start_index_map=(1,),
        operand_batching_dims=(0,),
        start_indices_batching_dims=(0,),
    )
    return lax.gather(
        table, index[..., None], dims, slice_sizes=(1, 1), mode=lax.GatherScatterMode.PROMISE_IN_BOUNDS
    )


def total(value):
    return jnp.sum(jnp.sum(value, axis=0, keepdims=True), axis=1, keepdims=True)


def split_terms(value):
    high = value.astype(jnp.bfloat16).astype(jnp.float32)
    return high, value - high


def contract_last(left, right):
    return lax.dot_general(
        left, right, (((1,), (1,)), ((), ())), preferred_element_type=jnp.float32
    )


def iota_rows(start, rows=16):
    return (lax.broadcasted_iota(jnp.int32, (rows, LANES), 0) + start).astype(jnp.float32).astype(jnp.bfloat16)


def wide_rows(row):
    return jnp.broadcast_to(row, (16, LANES)).astype(jnp.bfloat16)


def onehot(row, start):
    return jnp.where(row == iota_rows(start), jnp.bfloat16(1), jnp.bfloat16(0))


def place_row(block_shape, band, sub, values, row):
    rows = lax.broadcasted_iota(jnp.int32, block_shape, 0)
    lanes = lax.broadcasted_iota(jnp.int32, block_shape, 1)
    block = jnp.zeros(block_shape, jnp.float32)
    for k in range(5):
        block = jnp.where((rows == row) & (lanes == sub * 5 + k), values[k], block)
    return block


def place_scalars(block_shape, row, values):
    rows = lax.broadcasted_iota(jnp.int32, block_shape, 0)
    lanes = lax.broadcasted_iota(jnp.int32, block_shape, 1)
    block = jnp.zeros(block_shape, jnp.float32)
    for k, value in enumerate(values):
        block = jnp.where((rows == row) & (lanes == k), value, block)
    return block


def coarse_values(inverse_ref, modal_ref, band, sub):
    count = inverse_ref.shape[2]
    product = inverse_ref[band] * modal_ref[pl.ds(band, 1), 0:count]
    rows = lax.broadcasted_iota(jnp.int32, product.shape, 0)
    return [total(jnp.where(rows == sub * 5 + k, product, 0.0)) for k in range(5)]


def prepare_kernel(place_ref, rhs_ref, shift_ref, conn_ref, export_ref,
                   resid_ref, shift_out, conn_out, sent_ref, block_ref):
    band = place_ref[0]
    sub = place_ref[1]
    hi_rows = resid_ref.shape[1]
    for c in range(5):
        for h in range(hi_rows):
            resid_ref[c, h : h + 1, :] = rhs_ref[c : c + 1, h * WIDE : (h + 1) * WIDE]
            shift_out[c, h : h + 1, :] = shift_ref[c : c + 1, h * WIDE : (h + 1) * WIDE]
    for a in range(4):
        for h in range(conn_out.shape[1]):
            conn_out[a, h : h + 1, :] = conn_ref[a : a + 1, h * LANES : (h + 1) * LANES]
    gather_export(resid_ref, export_ref, sent_ref)
    modal = [total(resid_ref[c]) for c in range(5)]
    block_ref[...] = jnp.broadcast_to(
        place_row(block_ref.shape[1:], band, sub, modal, band)[None], block_ref.shape
    )


def gather_export(field_ref, export_ref, out_ref):
    halo = export_ref.shape[1]
    out_ref[...] = jnp.zeros(out_ref.shape, jnp.float32)
    parts = halo // LANES
    index = jnp.concatenate(
        [export_ref[:, g * LANES : (g + 1) * LANES] for g in range(parts)]
        + [jnp.zeros((8 - parts, LANES), jnp.int32)], axis=0)
    row = index >> 7
    low = index & 127
    found = [jnp.zeros((8, LANES), jnp.float32)] * 5
    for h in range(2 * field_ref.shape[1]):
        mask = row == h
        for c in range(5):
            table = jnp.broadcast_to(
                field_ref[c, h // 2 : h // 2 + 1, (h % 2) * LANES : (h % 2 + 1) * LANES], (8, LANES))
            found[c] = jnp.where(mask, lane_gather(table, low), found[c])
    for c in range(5):
        for g in range(parts):
            out_ref[c : c + 1, g * LANES : (g + 1) * LANES] = found[c][g : g + 1, :]


def laminate_kernel(place_ref, orient_ref, ids_ref, table_ref, rows_ref, dense_ref):
    band = place_ref[0]
    bands, _, per, count = orient_ref.shape
    layers = bands * per
    layups = table_ref.shape[1]
    thick = 1.0 / layers
    level = lax.broadcasted_iota(jnp.int32, (layers, LANES), 0).astype(jnp.float32)
    centre = (level + 0.5) * thick - 0.5
    square = centre * centre + thick * thick / 12.0
    rest = table_ref[...]
    terms = []
    for _ in range(3):
        terms.append(rest.astype(jnp.bfloat16))
        rest = rest - terms[-1].astype(jnp.float32)

    def step(i, carry):
        wide = pl.ds(pl.multiple_of(i * WIDE, WIDE), WIDE)
        choices = ids_ref[:, wide]
        chosen = lax.broadcasted_iota(jnp.int32, choices.shape, 0) == band
        ids = jnp.sum(jnp.where(chosen, choices, 0), axis=0, keepdims=True)
        picks = (lax.broadcasted_iota(jnp.int32, (layups, WIDE), 0) == ids).astype(jnp.float32).astype(jnp.bfloat16)
        coefs = sum(jnp.dot(term, picks, preferred_element_type=jnp.float32) for term in terms)
        for part in range(WIDE // LANES):
            cols = slice(part * LANES, (part + 1) * LANES)
            j = i * (WIDE // LANES) + part
            lanes = pl.ds(pl.multiple_of(j * LANES, LANES), LANES)
            first, double, ends, second, fourth, single, third, fifth = [
                coefs[q * layers : (q + 1) * layers, cols] for q in range(8)]
            comp_xx, comp_yy, comp_xy = [
                jnp.concatenate([orient_ref[b, m, :, lanes].astype(jnp.float32) for b in range(bands)], axis=0)
                for m in range(3)]
            scaled_x = first * comp_xx
            scaled_y = first * comp_yy
            both = comp_xx + comp_yy
            stiff = (
                (scaled_x + double) * comp_xx + ends,
                scaled_x * comp_yy + second * both + fourth,
                (scaled_y + double) * comp_yy + ends,
                comp_xy * (scaled_x + single),
                comp_xy * (scaled_y + single),
                first * comp_xy * comp_xy + third * both + fifth,
            )
            for q in range(6):
                sums = (
                    jnp.sum(stiff[q], axis=0, keepdims=True) * thick,
                    jnp.sum(stiff[q] * centre, axis=0, keepdims=True) * thick,
                    jnp.sum(stiff[q] * square, axis=0, keepdims=True) * thick,
                )
                for m in range(3):
                    row = m * 6 + q
                    rows_ref[row : row + 1, lanes] = sums[m]
                    dense_ref[row, pl.ds(j, 1), :] = sums[m]
        return carry

    lax.fori_loop(0, count // WIDE, step, 0)


def element_pass(z_ref, ghost_ref, lam_ref, conn_ref, force_ref, node_ref):
    tables = 2 * z_ref.shape[1]
    ghost_parts = ghost_ref.shape[1] // LANES
    elem_rows = conn_ref.shape[1]
    blocks = elem_rows // 8

    def gather_step(group, carry):
        corner = group // blocks
        block = group % blocks
        rows = pl.ds(pl.multiple_of(block * 8, 8), 8)
        index = conn_ref[corner, rows, :]
        row = index >> 7
        low = index & 127
        found = [jnp.zeros((8, LANES), jnp.float32)] * 5
        for h in range(tables + ghost_parts):
            mask = row == h
            for c in range(5):
                if h < tables:
                    source = z_ref[c, h // 2 : h // 2 + 1, (h % 2) * LANES : (h % 2 + 1) * LANES]
                else:
                    g = h - tables
                    source = ghost_ref[c : c + 1, g * LANES : (g + 1) * LANES]
                found[c] = jnp.where(mask, lane_gather(jnp.broadcast_to(source, (8, LANES)), low), found[c])
        for c in range(5):
            node_ref[corner * 5 + c, rows, :] = found[c]
        return carry

    lax.fori_loop(0, 4 * blocks, gather_step, 0)

    def force_step(block, carry):
        energy, held, lent = carry
        held, lent = list(held), list(lent)
        rows = pl.ds(pl.multiple_of(block * 8, 8), 8)
        node = [[node_ref[a * 5 + c, rows, :] for c in range(5)] for a in range(4)]

        def along_x(c):
            return 0.5 * ((node[1][c] - node[0][c]) + (node[2][c] - node[3][c]))

        def along_y(c):
            return 0.5 * ((node[2][c] - node[1][c]) + (node[3][c] - node[0][c]))

        def mean(c):
            return 0.25 * ((node[0][c] + node[1][c]) + (node[2][c] + node[3][c]))

        strain = (along_x(0), along_y(1), along_y(0) + along_x(1))
        curve = (along_x(3), along_y(4), along_y(3) + along_x(4))
        shear_one = along_x(2) + mean(3)
        shear_two = along_y(2) + mean(4)
        lam = [lam_ref[q, rows, :] for q in range(18)]

        def apply_sym(comps, vec):
            return (
                comps[0] * vec[0] + comps[1] * vec[1] + comps[3] * vec[2],
                comps[1] * vec[0] + comps[2] * vec[1] + comps[4] * vec[2],
                comps[3] * vec[0] + comps[4] * vec[1] + comps[5] * vec[2],
            )

        mem = apply_sym(lam[0:6], strain)
        mix = apply_sym(lam[6:12], curve)
        mix_two = apply_sym(lam[6:12], strain)
        bend = apply_sym(lam[12:18], curve)
        force = [mem[i] + mix[i] for i in range(3)]
        moment = [mix_two[i] + bend[i] for i in range(3)]
        stiff_s = shear_factor * lam[5]
        cut_one = stiff_s * shear_one
        cut_two = stiff_s * shear_two
        energy = energy + (force[0] * strain[0] + force[1] * strain[1] + force[2] * strain[2])
        energy = energy + (moment[0] * curve[0] + moment[1] * curve[1] + moment[2] * curve[2])
        energy = energy + (cut_one * shear_one + cut_two * shear_two)
        for a in range(4):
            values = (
                deriv_x[a] * force[0] + deriv_y[a] * force[2],
                deriv_y[a] * force[1] + deriv_x[a] * force[2],
                deriv_x[a] * cut_one + deriv_y[a] * cut_two,
                deriv_x[a] * moment[0] + deriv_y[a] * moment[2] + 0.25 * cut_one,
                deriv_y[a] * moment[1] + deriv_x[a] * moment[2] + 0.25 * cut_two,
            )
            base = (a * elem_rows + block * 8) * 16
            on_ghost = conn_ref[a, rows, :] >= tables * LANES
            for c in range(5):
                on = jnp.where(on_ghost, values[c], 0.0)
                lent[c] = lent[c] + on
                held[c] = held[c] + (values[c] - on)
                high, rest = split_terms(values[c])
                force_ref[pl.ds(base + c, 8, stride=16), :] = high
                force_ref[pl.ds(base + 5 + c, 8, stride=16), :] = rest
        return energy, tuple(held), tuple(lent)

    zero = jnp.zeros((8, LANES), jnp.float32)
    return lax.fori_loop(0, blocks, force_step, (zero, (zero,) * 5, (zero,) * 5))


def pair_chunk(high, low, terms, tile):
    high_row = wide_rows(high)
    low_row = wide_rows(low)
    pick = onehot(high_row, 0)
    left = [pick * wide_rows(term) for term in terms]
    if tile is not None:
        on_ghost = jnp.where(high_row == jnp.bfloat16(16), jnp.bfloat16(1), jnp.bfloat16(0))
        left.append(on_ghost * tile.astype(jnp.bfloat16))
    right = [onehot(low_row, j * 16) for j in range(WIDE // 16)]
    return jnp.concatenate(left, axis=0), jnp.concatenate(right, axis=0)


def scatter_kernel(last, place_ref, force_ref, conn_ref, z_ref, shift_ref, export_ref, own_ref, ghost_sum_ref, *rest):
    sent_ref = None if last else rest[0]
    acc_ref = rest[-1]
    blocks = conn_ref.shape[1] // 8
    acc_ref[...] = jnp.zeros(acc_ref.shape, jnp.float32)

    def step(corner, carry):
        left, right = [], []
        for block in range(blocks):
            index = conn_ref[corner, block * 8 : block * 8 + 8, :]
            high = (index >> 8).astype(jnp.float32)
            low = (index & 255).astype(jnp.float32)
            for q in range(8):
                start = pl.multiple_of(((corner * blocks + block) * 8 + q) * 16, 16)
                tile = force_ref[pl.ds(start, 16), :]
                one, two = pair_chunk(high[q : q + 1, :], low[q : q + 1, :],
                                      [tile[k : k + 1, :] for k in range(5 * SPLITS)], tile)
                left.append(one)
                right.append(two)
        acc_ref[...] += contract_last(jnp.concatenate(left, axis=1), jnp.concatenate(right, axis=1))
        return carry

    lax.fori_loop(0, 4, step, 0)
    for c in range(5):
        own_ref[c] = acc_ref[c * 16 : (c + 1) * 16] + acc_ref[(5 + c) * 16 : (6 + c) * 16] + shift_ref[c] * z_ref[c]
    ghost = acc_ref[160:165] + acc_ref[165:170]
    ghost_sum_ref[...] = jnp.concatenate([ghost, jnp.zeros((3, ghost.shape[1]), jnp.float32)], axis=0)
    if sent_ref is not None:
        gather_export(own_ref, export_ref, sent_ref)


def scatter_back(back_ref, export_ref, live):
    halo = export_ref.shape[1]
    left, right = [], []
    for q in range(halo // LANES):
        cols = slice(q * LANES, (q + 1) * LANES)
        index = export_ref[:, cols]
        values = [split_terms(jnp.where(live, back_ref[c : c + 1, cols], 0.0)) for c in range(5)]
        one, two = pair_chunk((index >> 8).astype(jnp.float32), (index & 255).astype(jnp.float32),
                              [values[c][t] for t in range(2) for c in range(5)], None)
        left.append(one)
        right.append(two)
    summed = contract_last(jnp.concatenate(left, axis=1), jnp.concatenate(right, axis=1))
    return [summed[c * 16 : (c + 1) * 16] + summed[(5 + c) * 16 : (6 + c) * 16] for c in range(5)]


def exchange_block(place, sums, z_ref, resid_ref, image_ref, shift_ref, block_ref):
    band, sub, bands = place
    energy, held_force, lent_force = sums
    modal = []
    square = jnp.zeros(z_ref.shape[1:], jnp.float32)
    with_resid = jnp.zeros(z_ref.shape[1:], jnp.float32)
    with_image = jnp.zeros(z_ref.shape[1:], jnp.float32)
    for c in range(5):
        z = z_ref[c]
        held = shift_ref[c] * z
        square = square + held * z
        with_resid = with_resid + resid_ref[c] * z
        if image_ref is not None:
            with_image = with_image + image_ref[c] * z
        modal.append(total(held) + total(held_force[c]))
    lower = [total(value) for value in lent_force]
    scalars = [total(energy) + total(square), total(with_image), total(with_resid)]
    shape = block_ref.shape[1:]
    block = place_row(shape, band, sub, modal, band)
    block = block + jnp.where(band > 0, place_row(shape, band, sub, lower, band - 1), 0.0)
    block = block + place_scalars(shape, bands, scalars)
    block_ref[...] = jnp.broadcast_to(block[None], block_ref.shape)


def begin_kernel(place_ref, blocks_ref, ghost_in, partner_ref, resid_ref, shift_ref, inverse_ref, lam_ref, conn_ref,
                 z_ref, force_ref, block_ref, ghost_resid_ref, state_ref, same_ref,
                 ghost_ref, node_ref):
    band, sub = place_ref[0], place_ref[1]
    bands = inverse_ref.shape[0]
    state_ref[...] = jnp.zeros(state_ref.shape, jnp.float32)
    state_ref[0] = jnp.sum(blocks_ref[...], axis=0)
    mine = coarse_values(inverse_ref, state_ref.at[0], band, sub)
    lower = coarse_values(inverse_ref, state_ref.at[0], jnp.maximum(band - 1, 0), sub)
    for c in range(5):
        z_ref[c] = resid_ref[c] + mine[c]
    ghost_resid_ref[...] = ghost_in[...]
    for c in range(5):
        value = ghost_in[c : c + 1, :] + lower[c]
        ghost_ref[c : c + 1, :] = jnp.where(band > 0, value, 0.0)
    halo = partner_ref.shape[1]
    spread = jnp.broadcast_to(partner_ref[...].astype(jnp.float32), (halo, halo))
    same_ref[...] = jnp.where(spread == spread.T, 1.0, 0.0).astype(jnp.bfloat16)
    sums = element_pass(z_ref, ghost_ref, lam_ref, conn_ref, force_ref, node_ref)
    exchange_block((band, sub, bands), sums, z_ref, resid_ref, None, shift_ref, block_ref)


def step_scalars(blocks_ref, state_ref, bands, first):
    block = jnp.sum(blocks_ref[...], axis=0)
    energy = block[bands : bands + 1, 0:1]
    cross = block[bands : bands + 1, 1:2]
    gamma = block[bands : bands + 1, 2:3]
    if first:
        return block, gamma, jnp.zeros_like(gamma), energy, gamma / energy
    beta = gamma / state_ref[2, 0:1, 0:1]
    curve = energy + 2.0 * beta * cross + beta * beta * state_ref[2, 1:2, 0:1]
    return block, gamma, beta, curve, gamma / curve


def advance_kernel(first, *refs):
    it = iter(refs)
    place_ref, blocks_ref, back_ref, got_ref = next(it), next(it), next(it), next(it)
    own_in, ghost_sum_in, z_in, resid_in, state_in, ghost_resid_in, same_ref = (next(it) for _ in range(7))
    if not first:
        dir_in, image_in, field_in, ghost_image_in = (next(it) for _ in range(4))
    shift_ref, inverse_ref, lam_ref, conn_ref, export_ref = (next(it) for _ in range(5))
    z_ref, resid_ref, dir_ref, image_ref, field_ref, force_ref = (next(it) for _ in range(6))
    block_ref, ghost_resid_ref, ghost_image_ref, state_ref = (next(it) for _ in range(4))
    ghost_ref, node_ref = (next(it) for _ in range(2))
    band, sub = place_ref[0], place_ref[1]
    bands = inverse_ref.shape[0]
    block, gamma, beta, curve, alpha = step_scalars(blocks_ref, state_in, bands, first)
    modal_image = block if first else block + beta * state_in[1]
    state_ref[1] = modal_image
    state_ref[0] = state_in[0] - alpha * modal_image
    state_ref[2] = jnp.zeros(state_ref.shape[1:], jnp.float32)
    state_ref[2, 0:1, :] = jnp.broadcast_to(gamma, (1, state_ref.shape[2]))
    state_ref[2, 1:2, :] = jnp.broadcast_to(curve, (1, state_ref.shape[2]))
    mine = coarse_values(inverse_ref, state_ref.at[0], band, sub)
    lower = coarse_values(inverse_ref, state_ref.at[0], jnp.maximum(band - 1, 0), sub)
    back = scatter_back(back_ref, export_ref, band < bands - 1)
    for c in range(5):
        image = own_in[c] + back[c]
        direction = z_in[c]
        if not first:
            image = image + beta * image_in[c]
            direction = direction + beta * dir_in[c]
        image_ref[c] = image
        dir_ref[c] = direction
        moved = alpha * direction
        field_ref[c] = moved if first else field_in[c] + moved
        resid = resid_in[c] - alpha * image
        resid_ref[c] = resid
        z_ref[c] = resid + mine[c]
    terms = split_terms(ghost_sum_in[...])
    same = same_ref[...]
    shared = sum(jnp.dot(term.astype(jnp.bfloat16), same, preferred_element_type=jnp.float32) for term in terms)
    ghost_image = got_ref[...] + shared
    if not first:
        ghost_image = ghost_image + beta * ghost_image_in[...]
    ghost_image_ref[...] = ghost_image
    ghost_resid = ghost_resid_in[...] - alpha * ghost_image
    ghost_resid_ref[...] = ghost_resid
    for c in range(5):
        value = ghost_resid[c : c + 1, :] + lower[c]
        ghost_ref[c : c + 1, :] = jnp.where(band > 0, value, 0.0)
    sums = element_pass(z_ref, ghost_ref, lam_ref, conn_ref, force_ref, node_ref)
    exchange_block((band, sub, bands), sums, z_ref, resid_ref, image_ref, shift_ref, block_ref)


def close_kernel(place_ref, blocks_ref, back_ref, own_in, z_in, resid_in, state_in, dir_in, image_in, field_in,
                 export_ref, field_ref, resid_ref):
    band = place_ref[0]
    bands = place_ref[2]
    last = blocks_ref.shape[1] - 1
    block, gamma, beta, curve, alpha = step_scalars(blocks_ref, state_in, last, False)
    back = scatter_back(back_ref, export_ref, band < bands - 1)
    for c in range(5):
        image = own_in[c] + back[c] + beta * image_in[c]
        direction = z_in[c] + beta * dir_in[c]
        field = field_in[c] + alpha * direction
        resid = resid_in[c] - alpha * image
        for h in range(field.shape[0]):
            field_ref[c : c + 1, h * WIDE : (h + 1) * WIDE] = field[h : h + 1, :]
            resid_ref[c : c + 1, h * WIDE : (h + 1) * WIDE] = resid[h : h + 1, :]


def call(kernel, name, outs, scratch, *args):
    shapes = [jax.ShapeDtypeStruct(*out) for out in outs]
    specs = [pl.BlockSpec(memory_space=pltpu.SMEM)] + [
        pl.BlockSpec(memory_space=pltpu.VMEM) for _ in args[1:]]
    return pl.pallas_call(
        kernel,
        out_shape=shapes,
        in_specs=specs,
        out_specs=[pl.BlockSpec(memory_space=pltpu.VMEM) for _ in outs],
        scratch_shapes=scratch,
        name=name,
        compiler_params=pltpu.CompilerParams(vmem_limit_bytes=GRANT),
    )(*args)


def ring(value, axis, step):
    count = lax.axis_size(axis)
    return lax.ppermute(value, axis, [(j, (j + step) % count) for j in range(count)])


def shards(
    orientation,
    layup_id,
    layup_table,
    grade_coefficients,
    connectivity,
    export_nodes,
    shift,
    rhs,
    coarse_inverse,
):
    f32 = jnp.float32
    bands = lax.axis_size("band")
    devices = bands * lax.axis_size("sub")
    nodes = rhs.shape[1]
    elements = connectivity.shape[1]
    halo = export_nodes.shape[0]
    hi_rows = nodes // WIDE
    coarse = coarse_inverse.shape[1]
    lanes = -(-coarse // LANES) * LANES
    block_shape = (devices, bands + 1, lanes)
    field_shape = (5, hi_rows, WIDE)
    place = jnp.stack([lax.axis_index("band"), lax.axis_index("sub"), jnp.int32(bands)]).astype(jnp.int32)

    packed, rhs = lax.optimization_barrier((orientation.transpose(2, 1, 0, 3), rhs))
    layers = lax.all_to_all(packed, "band", 0, 0, tiled=True)

    export = export_nodes.reshape(1, halo)
    resid, shift_d, conn, sent, block = call(
        prepare_kernel, "prepare",
        [(field_shape, f32), (field_shape, f32), ((4, elements // LANES, LANES), jnp.int32),
         ((8, halo), f32), (block_shape, f32)],
        [], place, rhs, shift, connectivity, export)
    got = ring(sent, "band", 1)
    partner = ring(export, "band", 1)
    blocks = lax.all_to_all(block, ("band", "sub"), 0, 0, tiled=True)

    per_layer = grade_coefficients[layup_table]
    b1, b2, b3, b4, b5 = (per_layer[:, :, q] for q in range(5))
    table = jnp.concatenate(
        [b1, 2.0 * b2 + 4.0 * b3, b4 + 2.0 * b5, b2, b4, b2 + 2.0 * b3, b3, b5], axis=1).T
    lam_rows, lam = call(
        laminate_kernel, "laminate",
        [((18, elements), f32), ((18, elements // LANES, LANES), f32)],
        [], place, layers, layup_id, table)

    rows = 5 * SPLITS * 16 + 16
    scratch = [pltpu.VMEM((8, halo), f32), pltpu.VMEM((20, elements // LANES, LANES), f32)]
    total_scratch = [pltpu.VMEM((rows, WIDE), f32)]
    field_out = (field_shape, f32)
    ghost_out = ((8, halo), f32)
    state_out = ((3, bands + 1, lanes), f32)
    force_out = ((4 * (elements // LANES) * 16, LANES), f32)
    block_out = (block_shape, f32)
    z, force, block, ghost_resid, state, same = call(
        begin_kernel, "begin",
        [field_out, force_out, block_out, ghost_out, state_out, ((halo, halo), jnp.bfloat16)],
        scratch, place, blocks, got, partner, resid, shift_d, coarse_inverse, lam, conn)

    direction = image = field = ghost_image = None
    for step in range(ITERS):
        first = step == 0
        last = step == ITERS - 1
        blocks = lax.all_to_all(block, ("band", "sub"), 0, 0, tiled=True)
        sums = call(
            functools.partial(scatter_kernel, last), f"scatter{step}",
            [field_out, ghost_out] + ([] if last else [ghost_out]),
            total_scratch, place, force, conn, z, shift_d, export)
        own, ghost_sum = sums[:2]
        back = ring(ghost_sum, "band", -1)
        if last:
            break
        got = ring(sums[2], "band", 1)
        past = [] if first else [direction, image, field, ghost_image]
        z, resid, direction, image, field, force, block, ghost_resid, ghost_image, state = call(
            functools.partial(advance_kernel, first), f"advance{step}",
            [field_out] * 5 + [force_out, block_out, ghost_out, ghost_out, state_out],
            scratch, place, blocks, back, got, own, ghost_sum, z, resid, state, ghost_resid, same,
            *past, shift_d, coarse_inverse, lam, conn, export)

    out_field, out_resid = call(
        close_kernel, "close", [((5, nodes), f32), ((5, nodes), f32)],
        [], place, blocks, back, own, z, resid, state, direction, image, field, export)
    return lam_rows, out_field, out_resid


def solution(mesh):
    placed = (
        P("band", None, None, "sub"),
        P(None, "sub"),
        P(),
        P(),
        P(None, ("band", "sub")),
        P(("band", "sub")),
        P(None, ("band", "sub")),
        P(None, ("band", "sub")),
        P(),
    )
    return jax.shard_map(
        shards,
        mesh=mesh,
        in_specs=placed,
        out_specs=(P(None, ("band", "sub")), P(None, ("band", "sub")), P(None, ("band", "sub"))),
        check_vma=False,
    )
```

```python
import functools

import jax
import jax.numpy as jnp
from jax import lax
from jax.experimental import pallas as pl
from jax.experimental.pallas import tpu as pltpu
from jax.sharding import PartitionSpec as P


ITERS = 3
LANES = 128
WIDE = 256
SPLITS = 2
GRANT = 20 * 1024 * 1024

deriv_x = (-0.5, 0.5, 0.5, -0.5)
deriv_y = (-0.5, -0.5, 0.5, 0.5)
shear_factor = 5.0 / 6.0


def lane_gather(table, index):
    dims = lax.GatherDimensionNumbers(
        offset_dims=(),
        collapsed_slice_dims=(1,),
        start_index_map=(1,),
        operand_batching_dims=(0,),
        start_indices_batching_dims=(0,),
    )
    return lax.gather(
        table, index[..., None], dims, slice_sizes=(1, 1), mode=lax.GatherScatterMode.PROMISE_IN_BOUNDS
    )


def total(value):
    return jnp.sum(jnp.sum(value, axis=0, keepdims=True), axis=1, keepdims=True)


def split_terms(value):
    high = value.astype(jnp.bfloat16).astype(jnp.float32)
    return high, value - high


def contract_last(left, right):
    return lax.dot_general(
        left, right, (((1,), (1,)), ((), ())), preferred_element_type=jnp.float32
    )


def iota_rows(start, rows=16):
    return (lax.broadcasted_iota(jnp.int32, (rows, LANES), 0) + start).astype(jnp.float32).astype(jnp.bfloat16)


def wide_rows(row):
    return jnp.broadcast_to(row, (16, LANES)).astype(jnp.bfloat16)


def onehot(row, start):
    return jnp.where(row == iota_rows(start), jnp.bfloat16(1), jnp.bfloat16(0))


def place_row(block_shape, sub, values, row):
    rows = lax.broadcasted_iota(jnp.int32, block_shape, 0)
    lanes = lax.broadcasted_iota(jnp.int32, block_shape, 1)
    block = jnp.zeros(block_shape, jnp.float32)
    for k in range(5):
        block = jnp.where((rows == row) & (lanes == sub * 5 + k), values[k], block)
    return block


def place_scalars(block_shape, row, values):
    rows = lax.broadcasted_iota(jnp.int32, block_shape, 0)
    lanes = lax.broadcasted_iota(jnp.int32, block_shape, 1)
    block = jnp.zeros(block_shape, jnp.float32)
    for k, value in enumerate(values):
        block = jnp.where((rows == row) & (lanes == k), value, block)
    return block


def coarse_values(inverse_ref, modal_ref, band, sub):
    count = inverse_ref.shape[2]
    product = inverse_ref[band] * modal_ref[pl.ds(band, 1), 0:count]
    rows = lax.broadcasted_iota(jnp.int32, product.shape, 0)
    return [total(jnp.where(rows == sub * 5 + k, product, 0.0)) for k in range(5)]


def prepare_kernel(place_ref, orient_hbm, rhs_hbm, export_hbm, shift_hbm, conn_hbm,
                   resid_ref, shift_out, conn_out, export_out, sent_ref, block_ref, *rest):
    slice_refs = rest[:-7]
    orient_ref, rhs_ref, export_ref, shift_ref, conn_ref, spread_ref, sems = rest[-7:]
    copies = [
        pltpu.make_async_copy(source, target, sems.at[i])
        for i, (source, target) in enumerate((
            (rhs_hbm, rhs_ref), (export_hbm, export_ref), (orient_hbm, orient_ref),
            (shift_hbm, shift_ref), (conn_hbm, conn_ref)))
    ]
    for copy in copies:
        copy.start()
    band = place_ref[0]
    sub = place_ref[1]
    copies[0].wait()
    copies[1].wait()
    hi_rows = resid_ref.shape[1]
    for c in range(5):
        for h in range(hi_rows):
            resid_ref[c, h : h + 1, :] = rhs_ref[c : c + 1, h * WIDE : (h + 1) * WIDE]
    gather_export(resid_ref, export_ref, sent_ref)
    sent_ref[5:6, :] = export_ref[...].astype(jnp.float32)
    export_out[...] = export_ref[...]
    modal = [total(resid_ref[c]) for c in range(5)]
    block_ref[...] = jnp.broadcast_to(place_row(block_ref.shape[1:], sub, modal, band)[None], block_ref.shape)
    copies[2].wait()
    per, comps, bands, count = orient_ref.shape
    chunks = count // LANES
    pitch = spread_ref.shape[0] // (per * comps * chunks)
    for m in range(comps):
        for k in range(per):
            plane = orient_ref[k, m].astype(jnp.float32)
            for j in range(chunks):
                row = ((j * comps + m) * per + k) * pitch
                spread_ref[row : row + bands, :] = plane[:, j * LANES : (j + 1) * LANES]
    for s, slice_ref in enumerate(slice_refs):
        target = lax.rem(band + bands - s, bands)
        for j in range(chunks):
            start = j * comps * per * pitch + target
            slice_ref[:, j * LANES : (j + 1) * LANES] = spread_ref[
                pl.ds(start, per * comps, stride=pitch), :].astype(jnp.bfloat16)
    copies[3].wait()
    for c in range(5):
        for h in range(hi_rows):
            shift_out[c, h : h + 1, :] = shift_ref[c : c + 1, h * WIDE : (h + 1) * WIDE]
    copies[4].wait()
    for a in range(4):
        for h in range(conn_out.shape[1]):
            conn_out[a, h : h + 1, :] = conn_ref[a : a + 1, h * LANES : (h + 1) * LANES]


def gather_export(field_ref, export_ref, out_ref):
    halo = export_ref.shape[1]
    out_ref[...] = jnp.zeros(out_ref.shape, jnp.float32)
    parts = halo // LANES
    index = jnp.concatenate(
        [export_ref[:, g * LANES : (g + 1) * LANES] for g in range(parts)]
        + [jnp.zeros((8 - parts, LANES), jnp.int32)], axis=0)
    row = index >> 7
    low = index & 127
    found = [jnp.zeros((8, LANES), jnp.float32)] * 5
    for h in range(2 * field_ref.shape[1]):
        mask = row == h
        for c in range(5):
            table = jnp.broadcast_to(
                field_ref[c, h // 2 : h // 2 + 1, (h % 2) * LANES : (h % 2 + 1) * LANES], (8, LANES))
            found[c] = jnp.where(mask, lane_gather(table, low), found[c])
    for c in range(5):
        for g in range(parts):
            out_ref[c : c + 1, g * LANES : (g + 1) * LANES] = found[c][g : g + 1, :]


def laminate_kernel(layers, place_ref, grade_ref, ids_ref, table_ref, *rest):
    slice_refs, (rows_ref, dense_ref) = rest[:-2], rest[-2:]
    band = place_ref[0]
    per = layers // len(slice_refs)
    count = ids_ref.shape[1]
    layups = table_ref.shape[0]
    span = 2 * WIDE
    thick = 1.0 / layers
    level = lax.rem(lax.broadcasted_iota(jnp.int32, (layers, LANES), 0) + band * per, layers).astype(jnp.float32)
    centre = (level + 0.5) * thick - 0.5
    square = centre * centre + thick * thick / 12.0

    lane = lax.broadcasted_iota(jnp.int32, (layups, LANES), 1)
    grades = jnp.concatenate(
        [table_ref[...], jnp.zeros((layups, LANES - layers), jnp.int32)], axis=1).astype(jnp.float32)
    grades = lane_gather(grades, lax.rem(lane + band * per, layers))
    kind = lane // layers
    rest_table = jnp.zeros((layups, LANES), jnp.float32)
    for g in range(grade_ref.shape[0]):
        b1, b2, b3, b4, b5 = (grade_ref[g, q] for q in range(5))
        coefs = (b1, 2.0 * b2 + 4.0 * b3, b4 + 2.0 * b5, b2, b4, b2 + 2.0 * b3, b3, b5)
        line = jnp.zeros((layups, LANES), jnp.float32)
        for q in range(8):
            line = jnp.where(kind == q, coefs[q], line)
        rest_table = jnp.where(grades == g, line, rest_table)
    rest_table = rest_table.T
    terms = []
    for _ in range(3):
        terms.append(rest_table.astype(jnp.bfloat16))
        rest_table = rest_table - terms[-1].astype(jnp.float32)

    def step(i, carry):
        wide = pl.ds(pl.multiple_of(i * span, span), span)
        choices = ids_ref[:, wide]
        chosen = lax.broadcasted_iota(jnp.int32, choices.shape, 0) == band
        ids = jnp.sum(jnp.where(chosen, choices, 0), axis=0, keepdims=True)
        picks = (lax.broadcasted_iota(jnp.int32, (layups, span), 0) == ids).astype(jnp.float32).astype(jnp.bfloat16)
        coefs = sum(jnp.dot(term, picks, preferred_element_type=jnp.float32) for term in terms)
        for part in range(span // LANES):
            cols = slice(part * LANES, (part + 1) * LANES)
            j = i * (span // LANES) + part
            lanes = pl.ds(pl.multiple_of(j * LANES, LANES), LANES)
            first, double, ends, second, fourth, single, third, fifth = [
                coefs[q * layers : (q + 1) * layers, cols] for q in range(8)]
            slices = [ref[:, lanes].astype(jnp.float32) for ref in slice_refs]
            comp_xx, comp_yy, comp_xy = [
                jnp.concatenate([part_of[m * per : (m + 1) * per] for part_of in slices], axis=0)
                for m in range(3)]
            scaled_x = first * comp_xx
            scaled_y = first * comp_yy
            both = comp_xx + comp_yy
            stiff = (
                (scaled_x + double) * comp_xx + ends,
                scaled_x * comp_yy + second * both + fourth,
                (scaled_y + double) * comp_yy + ends,
                comp_xy * (scaled_x + single),
                comp_xy * (scaled_y + single),
                first * comp_xy * comp_xy + third * both + fifth,
            )
            for q in range(6):
                sums = (
                    jnp.sum(stiff[q], axis=0, keepdims=True) * thick,
                    jnp.sum(stiff[q] * centre, axis=0, keepdims=True) * thick,
                    jnp.sum(stiff[q] * square, axis=0, keepdims=True) * thick,
                )
                for m in range(3):
                    row = m * 6 + q
                    rows_ref[row : row + 1, lanes] = sums[m]
                    dense_ref[row, pl.ds(j, 1), :] = sums[m]
        return carry

    lax.fori_loop(0, count // span, step, 0)


def view_matvec(z_ref, ghost_ref, lam_ref, conn_ref, force_ref, acc_ref):
    tables = 2 * z_ref.shape[1]
    ghost_parts = ghost_ref.shape[1] // LANES
    blocks = conn_ref.shape[1] // 8

    def rows_of(block):
        return pl.ds(pl.multiple_of(block * 8, 8), 8)

    def gather_block(block):
        node = []
        for a in range(4):
            index = conn_ref[a, rows_of(block), :]
            row = index >> 7
            low = index & 127
            found = [jnp.zeros((8, LANES), jnp.float32)] * 5
            for h in range(tables + ghost_parts):
                mask = row == h
                for c in range(5):
                    if h < tables:
                        source = z_ref[c, h // 2 : h // 2 + 1, (h % 2) * LANES : (h % 2 + 1) * LANES]
                    else:
                        g = h - tables
                        source = ghost_ref[c : c + 1, g * LANES : (g + 1) * LANES]
                    found[c] = jnp.where(mask, lane_gather(jnp.broadcast_to(source, (8, LANES)), low), found[c])
            node.append(found)
        return node

    def force_block(block, node, carry):
        energy, held, lent = carry
        held, lent = list(held), list(lent)
        rows = rows_of(block)

        def along_x(c):
            return 0.5 * ((node[1][c] - node[0][c]) + (node[2][c] - node[3][c]))

        def along_y(c):
            return 0.5 * ((node[2][c] - node[1][c]) + (node[3][c] - node[0][c]))

        def mean(c):
            return 0.25 * ((node[0][c] + node[1][c]) + (node[2][c] + node[3][c]))

        strain = (along_x(0), along_y(1), along_y(0) + along_x(1))
        curve = (along_x(3), along_y(4), along_y(3) + along_x(4))
        shear_one = along_x(2) + mean(3)
        shear_two = along_y(2) + mean(4)
        lam = [lam_ref[q, rows, :] for q in range(18)]

        def apply_sym(comps, vec):
            return (
                comps[0] * vec[0] + comps[1] * vec[1] + comps[3] * vec[2],
                comps[1] * vec[0] + comps[2] * vec[1] + comps[4] * vec[2],
                comps[3] * vec[0] + comps[4] * vec[1] + comps[5] * vec[2],
            )

        mem = apply_sym(lam[0:6], strain)
        mix = apply_sym(lam[6:12], curve)
        mix_two = apply_sym(lam[6:12], strain)
        bend = apply_sym(lam[12:18], curve)
        force = [mem[i] + mix[i] for i in range(3)]
        moment = [mix_two[i] + bend[i] for i in range(3)]
        stiff_s = shear_factor * lam[5]
        cut_one = stiff_s * shear_one
        cut_two = stiff_s * shear_two
        energy = energy + (force[0] * strain[0] + force[1] * strain[1] + force[2] * strain[2])
        energy = energy + (moment[0] * curve[0] + moment[1] * curve[1] + moment[2] * curve[2])
        energy = energy + (cut_one * shear_one + cut_two * shear_two)
        for a in range(4):
            values = (
                deriv_x[a] * force[0] + deriv_y[a] * force[2],
                deriv_y[a] * force[1] + deriv_x[a] * force[2],
                deriv_x[a] * cut_one + deriv_y[a] * cut_two,
                deriv_x[a] * moment[0] + deriv_y[a] * moment[2] + 0.25 * cut_one,
                deriv_y[a] * moment[1] + deriv_x[a] * moment[2] + 0.25 * cut_two,
            )
            on_ghost = conn_ref[a, rows, :] >= tables * LANES
            for c in range(5):
                on = jnp.where(on_ghost, values[c], 0.0)
                lent[c] = lent[c] + on
                held[c] = held[c] + (values[c] - on)
                terms = split_terms(values[c])
                for t in range(2):
                    force_ref[pl.ds(a * 128 + t * 5 + c, 8, stride=16), :] = terms[t]
        return energy, tuple(held), tuple(lent)

    def sum_block(block):
        left, right = [], []
        for a in range(4):
            index = conn_ref[a, rows_of(block), :]
            high = (index >> 8).astype(jnp.float32)
            low = (index & 255).astype(jnp.float32)
            for q in range(8):
                tile = force_ref[(a * 8 + q) * 16 : (a * 8 + q + 1) * 16, :]
                one, two = pair_chunk(high[q : q + 1, :], low[q : q + 1, :],
                                      [tile[k : k + 1, :] for k in range(10)], tile)
                left.append(one)
                right.append(two)
        return contract_last(jnp.concatenate(left, axis=1), jnp.concatenate(right, axis=1))

    zero = jnp.zeros((8, LANES), jnp.float32)
    acc_ref[...] = jnp.zeros(acc_ref.shape, jnp.float32)
    carry = force_block(0, gather_block(0), (zero, (zero,) * 5, (zero,) * 5))

    def step(block, carry):
        summed = sum_block(block)
        node = gather_block(block + 1)
        acc_ref[...] += summed
        return force_block(block + 1, node, carry)

    carry = lax.fori_loop(0, blocks - 1, step, carry)
    acc_ref[...] += sum_block(blocks - 1)
    return carry


def pair_chunk(high, low, terms, tile):
    high_row = wide_rows(high)
    low_row = wide_rows(low)
    pick = onehot(high_row, 0)
    left = [pick * wide_rows(term) for term in terms]
    if tile is not None:
        on_ghost = jnp.where(high_row == jnp.bfloat16(16), jnp.bfloat16(1), jnp.bfloat16(0))
        left.append(on_ghost * tile.astype(jnp.bfloat16))
    right = [onehot(low_row, j * 16) for j in range(WIDE // 16)]
    return jnp.concatenate(left, axis=0), jnp.concatenate(right, axis=0)


def finish_matvec(place, sums, z_ref, resid_ref, image_ref, shift_ref, export_ref, acc_ref,
                  own_ref, ghost_sum_ref, sent_ref, block_ref):
    for c in range(5):
        own_ref[c] = acc_ref[c * 16 : (c + 1) * 16] + acc_ref[(5 + c) * 16 : (6 + c) * 16] + shift_ref[c] * z_ref[c]
    ghost = acc_ref[160:165] + acc_ref[165:170]
    ghost_sum_ref[...] = jnp.concatenate([ghost, jnp.zeros((3, ghost.shape[1]), jnp.float32)], axis=0)
    if sent_ref is not None:
        gather_export(own_ref, export_ref, sent_ref)
    exchange_block(place, sums, z_ref, resid_ref, image_ref, shift_ref, block_ref)


def scatter_back(back_ref, export_ref, live):
    halo = export_ref.shape[1]
    left, right = [], []
    for q in range(halo // LANES):
        cols = slice(q * LANES, (q + 1) * LANES)
        index = export_ref[:, cols]
        values = [split_terms(jnp.where(live, back_ref[c : c + 1, cols], 0.0)) for c in range(5)]
        one, two = pair_chunk((index >> 8).astype(jnp.float32), (index & 255).astype(jnp.float32),
                              [values[c][t] for t in range(2) for c in range(5)], None)
        left.append(one)
        right.append(two)
    summed = contract_last(jnp.concatenate(left, axis=1), jnp.concatenate(right, axis=1))
    return [summed[c * 16 : (c + 1) * 16] + summed[(5 + c) * 16 : (6 + c) * 16] for c in range(5)]


def exchange_block(place, sums, z_ref, resid_ref, image_ref, shift_ref, block_ref):
    band, sub, bands = place
    energy, held_force, lent_force = sums
    modal = []
    square = jnp.zeros(z_ref.shape[1:], jnp.float32)
    with_resid = jnp.zeros(z_ref.shape[1:], jnp.float32)
    with_image = jnp.zeros(z_ref.shape[1:], jnp.float32)
    for c in range(5):
        z = z_ref[c]
        held = shift_ref[c] * z
        square = square + held * z
        with_resid = with_resid + resid_ref[c] * z
        if image_ref is not None:
            with_image = with_image + image_ref[c] * z
        modal.append(total(held) + total(held_force[c]))
    lower = [total(value) for value in lent_force]
    scalars = [total(energy) + total(square), total(with_image), total(with_resid)]
    shape = block_ref.shape[1:]
    block = place_row(shape, sub, modal, band)
    block = block + jnp.where(band > 0, place_row(shape, sub, lower, band - 1), 0.0)
    block = block + place_scalars(shape, bands, scalars)
    block_ref[...] = jnp.broadcast_to(block[None], block_ref.shape)


def begin_kernel(place_ref, blocks_ref, ghost_in, resid_ref, shift_ref, inverse_ref, lam_ref, conn_ref, export_ref,
                 z_ref, own_ref, ghost_sum_ref, sent_ref, block_ref, ghost_resid_ref, state_ref, same_ref,
                 ghost_ref, force_ref, acc_ref):
    band, sub = place_ref[0], place_ref[1]
    bands = inverse_ref.shape[0]
    state_ref[...] = jnp.zeros(state_ref.shape, jnp.float32)
    state_ref[0] = jnp.sum(blocks_ref[...], axis=0)
    mine = coarse_values(inverse_ref, state_ref.at[0], band, sub)
    lower = coarse_values(inverse_ref, state_ref.at[0], jnp.maximum(band - 1, 0), sub)
    for c in range(5):
        z_ref[c] = resid_ref[c] + mine[c]
    ghost_resid_ref[...] = ghost_in[...]
    ghost_resid_ref[5:6, :] = jnp.zeros((1, ghost_in.shape[1]), jnp.float32)
    for c in range(5):
        value = ghost_in[c : c + 1, :] + lower[c]
        ghost_ref[c : c + 1, :] = jnp.where(band > 0, value, 0.0)
    halo = ghost_in.shape[1]
    spread = jnp.broadcast_to(ghost_in[5:6, :], (halo, halo))
    same_ref[...] = jnp.where(spread == spread.T, 1.0, 0.0).astype(jnp.bfloat16)
    sums = view_matvec(z_ref, ghost_ref, lam_ref, conn_ref, force_ref, acc_ref)
    finish_matvec((band, sub, bands), sums, z_ref, resid_ref, None, shift_ref, export_ref, acc_ref,
                  own_ref, ghost_sum_ref, sent_ref, block_ref)


def step_scalars(blocks_ref, state_ref, bands, first):
    block = jnp.sum(blocks_ref[...], axis=0)
    energy = block[bands : bands + 1, 0:1]
    cross = block[bands : bands + 1, 1:2]
    gamma = block[bands : bands + 1, 2:3]
    if first:
        return block, gamma, jnp.zeros_like(gamma), energy, gamma / energy
    beta = gamma / state_ref[2, 0:1, 0:1]
    curve = energy + 2.0 * beta * cross + beta * beta * state_ref[2, 1:2, 0:1]
    return block, gamma, beta, curve, gamma / curve


def advance_kernel(first, send, *refs):
    it = iter(refs)
    place_ref, blocks_ref, back_ref, got_ref = next(it), next(it), next(it), next(it)
    own_in, ghost_sum_in, z_in, resid_in, state_in, ghost_resid_in, same_ref = (next(it) for _ in range(7))
    if not first:
        dir_in, image_in, field_in, ghost_image_in = (next(it) for _ in range(4))
    shift_ref, inverse_ref, lam_ref, conn_ref, export_ref = (next(it) for _ in range(5))
    z_ref, resid_ref, dir_ref, image_ref, field_ref, own_ref, ghost_sum_ref = (next(it) for _ in range(7))
    sent_ref = next(it) if send else None
    block_ref, ghost_resid_ref, ghost_image_ref, state_ref = (next(it) for _ in range(4))
    ghost_ref, force_ref, acc_ref = (next(it) for _ in range(3))
    band, sub = place_ref[0], place_ref[1]
    bands = inverse_ref.shape[0]
    block, gamma, beta, curve, alpha = step_scalars(blocks_ref, state_in, bands, first)
    modal_image = block if first else block + beta * state_in[1]
    state_ref[1] = modal_image
    state_ref[0] = state_in[0] - alpha * modal_image
    state_ref[2] = jnp.zeros(state_ref.shape[1:], jnp.float32)
    state_ref[2, 0:1, :] = jnp.broadcast_to(gamma, (1, state_ref.shape[2]))
    state_ref[2, 1:2, :] = jnp.broadcast_to(curve, (1, state_ref.shape[2]))
    mine = coarse_values(inverse_ref, state_ref.at[0], band, sub)
    lower = coarse_values(inverse_ref, state_ref.at[0], jnp.maximum(band - 1, 0), sub)
    back = scatter_back(back_ref, export_ref, band < bands - 1)
    for c in range(5):
        image = own_in[c] + back[c]
        direction = z_in[c]
        if not first:
            image = image + beta * image_in[c]
            direction = direction + beta * dir_in[c]
        image_ref[c] = image
        dir_ref[c] = direction
        moved = alpha * direction
        field_ref[c] = moved if first else field_in[c] + moved
        resid = resid_in[c] - alpha * image
        resid_ref[c] = resid
        z_ref[c] = resid + mine[c]
    terms = split_terms(ghost_sum_in[...])
    same = same_ref[...]
    shared = sum(jnp.dot(term.astype(jnp.bfloat16), same, preferred_element_type=jnp.float32) for term in terms)
    ghost_image = got_ref[...] + shared
    if not first:
        ghost_image = ghost_image + beta * ghost_image_in[...]
    ghost_image_ref[...] = ghost_image
    ghost_resid = ghost_resid_in[...] - alpha * ghost_image
    ghost_resid_ref[...] = ghost_resid
    for c in range(5):
        value = ghost_resid[c : c + 1, :] + lower[c]
        ghost_ref[c : c + 1, :] = jnp.where(band > 0, value, 0.0)
    sums = view_matvec(z_ref, ghost_ref, lam_ref, conn_ref, force_ref, acc_ref)
    finish_matvec((band, sub, bands), sums, z_ref, resid_ref, image_ref, shift_ref, export_ref, acc_ref,
                  own_ref, ghost_sum_ref, sent_ref, block_ref)


def close_kernel(place_ref, blocks_ref, back_ref, own_in, z_in, resid_in, state_in, dir_in, image_in, field_in,
                 export_ref, field_ref, resid_ref):
    band = place_ref[0]
    bands = place_ref[2]
    last = blocks_ref.shape[1] - 1
    _, _, beta, _, alpha = step_scalars(blocks_ref, state_in, last, False)
    back = scatter_back(back_ref, export_ref, band < bands - 1)
    for c in range(5):
        image = own_in[c] + back[c] + beta * image_in[c]
        direction = z_in[c] + beta * dir_in[c]
        field = field_in[c] + alpha * direction
        resid = resid_in[c] - alpha * image
        for h in range(field.shape[0]):
            field_ref[c : c + 1, h * WIDE : (h + 1) * WIDE] = field[h : h + 1, :]
            resid_ref[c : c + 1, h * WIDE : (h + 1) * WIDE] = resid[h : h + 1, :]


def call(kernel, outs, scratch, *args, scalars=1, in_hbm=False):
    shapes = [jax.ShapeDtypeStruct(*out) for out in outs]
    rest = pltpu.MemorySpace.HBM if in_hbm else pltpu.VMEM
    specs = [pl.BlockSpec(memory_space=pltpu.SMEM if i < scalars else rest) for i in range(len(args))]
    return pl.pallas_call(
        kernel,
        out_shape=shapes,
        in_specs=specs,
        out_specs=[pl.BlockSpec(memory_space=pltpu.VMEM) for _ in outs],
        scratch_shapes=scratch,
        compiler_params=pltpu.CompilerParams(vmem_limit_bytes=GRANT),
    )(*args)


def ring(value, axis, step):
    count = lax.axis_size(axis)
    return lax.ppermute(value, axis, [(j, (j + step) % count) for j in range(count)])


def shards(
    orientation,
    layup_id,
    layup_table,
    grade_coefficients,
    connectivity,
    export_nodes,
    shift,
    rhs,
    coarse_inverse,
):
    f32 = jnp.float32
    bands = lax.axis_size("band")
    devices = bands * lax.axis_size("sub")
    nodes = rhs.shape[1]
    elements = connectivity.shape[1]
    halo = export_nodes.shape[0]
    hi_rows = nodes // WIDE
    coarse = coarse_inverse.shape[1]
    lanes = -(-coarse // LANES) * LANES
    block_shape = (devices, bands + 1, lanes)
    field_shape = (5, hi_rows, WIDE)
    place = jnp.stack([lax.axis_index("band"), lax.axis_index("sub"), jnp.int32(bands)]).astype(jnp.int32)

    per, comps = orientation.shape[:2]
    layers = per * bands
    pitch = -(-bands // 8) * 8
    slice_out = ((per * comps, elements), jnp.bfloat16)
    export = export_nodes.reshape(1, halo)
    sources = (orientation, rhs, export, shift, connectivity)
    resid, shift_d, conn, export_d, sent, block, *slices = call(
        prepare_kernel,
        [(field_shape, f32), (field_shape, f32), ((4, elements // LANES, LANES), jnp.int32),
         ((1, halo), jnp.int32), ((8, halo), f32), (block_shape, f32)] + [slice_out] * bands,
        [pltpu.VMEM(value.shape, value.dtype) for value in sources]
        + [pltpu.VMEM((per * comps * pitch * (elements // LANES), LANES), f32),
           pltpu.SemaphoreType.DMA((len(sources),))],
        place, *(pltpu.with_memory_space_constraint(value, pltpu.MemorySpace.HBM) for value in sources), in_hbm=True)
    slices = [slices[0]] + [ring(slices[s], "band", -s) for s in range(1, bands)]
    got = ring(sent, "band", 1)
    blocks = lax.all_to_all(block, ("band", "sub"), 0, 0, tiled=True)
    lam_rows, lam = call(
        functools.partial(laminate_kernel, layers),
        [((18, elements), f32), ((18, elements // LANES, LANES), f32)],
        [], place, grade_coefficients, layup_id, layup_table, *slices, scalars=2)

    rows = 5 * SPLITS * 16 + 16
    scratch = [pltpu.VMEM((8, halo), f32), pltpu.VMEM((4 * 8 * 16, LANES), f32), pltpu.VMEM((rows, WIDE), f32)]
    field_out = (field_shape, f32)
    ghost_out = ((8, halo), f32)
    state_out = ((3, bands + 1, lanes), f32)
    block_out = (block_shape, f32)
    z, own, ghost_sum, sent, block, ghost_resid, state, same = call(
        begin_kernel,
        [field_out, field_out, ghost_out, ghost_out, block_out, ghost_out, state_out, ((halo, halo), jnp.bfloat16)],
        scratch, place, blocks, got, resid, shift_d, coarse_inverse, lam, conn, export_d)

    direction = image = field = ghost_image = None
    for step in range(ITERS - 1):
        first = step == 0
        send = step < ITERS - 2
        back = ring(ghost_sum, "band", -1)
        got = ring(sent, "band", 1)
        blocks = lax.all_to_all(block, ("band", "sub"), 0, 0, tiled=True)
        past = [] if first else [direction, image, field, ghost_image]
        made = call(
            functools.partial(advance_kernel, first, send),
            [field_out] * 6 + [ghost_out] * (2 if send else 1) + [block_out, ghost_out, ghost_out, state_out],
            scratch, place, blocks, back, got, own, ghost_sum, z, resid, state, ghost_resid, same,
            *past, shift_d, coarse_inverse, lam, conn, export_d)
        z, resid, direction, image, field, own, ghost_sum = made[:7]
        sent = made[7] if send else None
        block, ghost_resid, ghost_image, state = made[-4:]

    back = ring(ghost_sum, "band", -1)
    blocks = lax.all_to_all(block, ("band", "sub"), 0, 0, tiled=True)
    out_field, out_resid = call(
        close_kernel, [((5, nodes), f32), ((5, nodes), f32)],
        [], place, blocks, back, own, z, resid, state, direction, image, field, export_d)
    return lam_rows, out_field, out_resid


def solution(mesh):
    placed = (
        P("band", None, None, "sub"),
        P(None, "sub"),
        P(),
        P(),
        P(None, ("band", "sub")),
        P(("band", "sub")),
        P(None, ("band", "sub")),
        P(None, ("band", "sub")),
        P(),
    )
    return jax.shard_map(
        shards,
        mesh=mesh,
        in_specs=placed,
        out_specs=(P(None, ("band", "sub")), P(None, ("band", "sub")), P(None, ("band", "sub"))),
        check_vma=False,
    )
```
